32 devices in a mesh: dp: 8 (over y, x, core), tp: 4 (over z).
Axes of the slice: x: 2, y: 2, z: 4, core: 2. Of those that a mesh axis runs over, the one named last changes fastest.
Arguments:
- feats: bfloat16 [16, 256, 1024], P('dp', 'tp'), may hold values from -12 to 12
- noise: bfloat16 [16, 256, 1024], P('dp', 'tp'), may hold values from -0.59765625 to 0.59765625
- starts: int32 [16, 4], P('dp'), may hold values from 0 to 255
- span_length: int32 [16], P('dp'), may hold values from 1 to 25, as said below
- cotangent: bfloat16 [16, 256, 1024], P('dp', 'tp'), may hold values from -6 to 6
- norm_gains: float32 [5, 1024], replicated, may hold values from 0.1 to 1.9
- ffn1_in: bfloat16 [1024, 4096], P('dp', 'tp'), may hold values from -0.1875 to 0.1875
- ffn1_out: bfloat16 [1024, 4096], P('dp', 'tp'), may hold values from -0.09375 to 0.09375
- qkv_weight: bfloat16 [1024, 3, 1024], P('dp', None, 'tp'), may hold values from -0.1875 to 0.1875
- attn_out: bfloat16 [1024, 1024], P('dp', 'tp'), may hold values from -1.5 to 1.5
- conv_in: bfloat16 [1024, 2, 1024], P('dp', None, 'tp'), may hold values from -0.1875 to 0.1875
- conv_kernel: float32 [5, 1024], replicated, may hold values from -2.5 to 2.5
- batch_gain: float32 [1024], P('tp'), may hold values from 0.1 to 1.9
- batch_bias: float32 [1024], P('tp'), may hold values from -3 to 3
- conv_out: bfloat16 [1024, 1024], P('dp', 'tp'), may hold values from -0.1875 to 0.1875
- ffn2_in: bfloat16 [1024, 4096], P('dp', 'tp'), may hold values from -0.1875 to 0.1875
- ffn2_out: bfloat16 [1024, 4096], P('dp', 'tp'), may hold values from -0.09375 to 0.09375
Outputs:
- layer_out: float32 [16, 256, 1024], P('dp', 'tp')
- feats_grad: float32 [16, 256, 1024], P('dp', 'tp')
- masked_count: float32 [], replicated
- norm_gains_grad: float32 [5, 1024], replicated
- ffn1_in_grad: float32 [1024, 4096], P('dp', 'tp')
- ffn1_out_grad: float32 [1024, 4096], P('dp', 'tp')
- qkv_grad: float32 [1024, 3, 1024], P('dp', None, 'tp')
- attn_out_grad: float32 [1024, 1024], P('dp', 'tp')
- conv_in_grad: float32 [1024, 2, 1024], P('dp', None, 'tp')
- kernel_grad: float32 [5, 1024], replicated
- batch_gain_grad: float32 [1024], P('tp')
- batch_bias_grad: float32 [1024], P('tp')
- conv_out_grad: float32 [1024, 1024], P('dp', 'tp')
- ffn2_in_grad: float32 [1024, 4096], P('dp', 'tp')
- ffn2_out_grad: float32 [1024, 4096], P('dp', 'tp')
The draws below stay inside these ranges and needn't reach their ends.
Inputs may be any that keep to these rules, and one draw needn't show every extreme that they name: `span_length`: one item has span length 25.
All inputs are finite; a program needn't handle non-finite values.
Results may differ from the reference program's by a relative error of at most 0.02.
Values may be sent and summed in bfloat16 or wider, within the bound.
No kernel may reach another device: no remote copies, remote signals or barrier semaphores. Data moves between devices by JAX's collectives and lax.ppermute only.
A program may use at most 128 MiB of HBM per device.

```python
import jax
import jax.numpy as jnp
from jax import lax

D = 1024
FF = 4096
HEADS = 8
HEAD_DIM = 128
KERNEL = 5
NORMS = 5
FRAMES = 256
SPANS = 4
MAX_SPAN = 25
ITEMS = 2
ITEMS_ALL = 16
TOKENS = 4096
N_DP = 8


def draw_feats(key, part):
    base_key, vector_key = jax.random.split(jax.random.fold_in(key, 11))
    shape = (ITEMS_ALL, FRAMES, D)
    jitter = jax.random.normal(base_key, shape, jnp.float32)
    direction = jax.random.normal(vector_key, (ITEMS_ALL, 1, D), jnp.float32)
    growth = 2.0 * (jnp.arange(ITEMS_ALL, dtype=jnp.float32)[:, None, None] + 1.0) / ITEMS_ALL
    return jnp.clip(jitter + growth * direction, -12.0, 12.0).astype(jnp.bfloat16)


def draw_span_length(key, part):
    order = jnp.arange(ITEMS_ALL, dtype=jnp.int32)
    ceiling = jnp.maximum(1 + (MAX_SPAN - 1) * (order + 1) // ITEMS_ALL, 2)
    drawn = jnp.minimum(1 + jax.random.randint(jax.random.fold_in(key, 23), (ITEMS_ALL,), 0, ceiling), MAX_SPAN)
    return jnp.where(order == ITEMS_ALL - 1, MAX_SPAN, drawn).astype(jnp.int32)


def place_ends(entries, rng, least, high):
    index_at = [jax.random.randint(jax.random.fold_in(rng, axis), (), 0, length) for axis, length in enumerate(entries.shape)]
    longest = entries.shape.index(max(entries.shape))
    neighbour = index_at[:longest] + [(index_at[longest] + 1) % entries.shape[longest]] + index_at[longest + 1:]
    return entries.at[tuple(index_at)].set(least).at[tuple(neighbour)].set(high)


def spiked(entries, key, source, target, parts, factor):
    owner, partner = [(jnp.arange(entries.shape[axis_at]) // (entries.shape[axis_at] // parts)).reshape([-1 if axis == axis_at else 1 for axis in range(entries.ndim)]) for axis_at in (source, target)]
    chosen = jax.random.permutation(key, parts)[partner]
    strong = (owner == chosen) | (owner == (partner + parts // 2) % parts)
    return jnp.where(strong, factor * entries, entries)


def steps_of(key, dims, pieces, least, high):
    loudness = 1.0
    for dim, shards_of in pieces:
        heights = jax.random.uniform(jax.random.fold_in(jax.random.fold_in(key, 6), dim), (shards_of,), jnp.float32, least / len(pieces), high / len(pieces))
        loudness = loudness * jnp.repeat(jnp.exp(heights), dims[dim] // shards_of).reshape((-1,) + (1,) * (len(dims) - 1 - dim))
    return loudness


def scatter_about(own_key, dims, scale, bound, shards=(), held_as=jnp.bfloat16):
    loudness = steps_of(own_key, dims, shards, -0.22, 0.18) if shards else 1.0
    result = jax.random.normal(own_key, dims, jnp.float32) * scale * loudness
    return jnp.minimum(jnp.maximum(result, -bound), bound).astype(held_as)


def bell_draw_with(key, dims, scale, most, cuts, heavy, kind=jnp.bfloat16):
    values = scale * jax.random.normal(key, dims, jnp.float32)
    if cuts:
        values = values * steps_of(key, dims, cuts, -0.22, 0.18)
    return jnp.clip(spiked(values, jax.random.fold_in(key, 3), *heavy), -most, most).astype(kind)


def setup_inputs(seed: int = 0) -> dict:
    key_of = jax.random.split(jax.random.key(seed), 18)
    return {
        "feats": draw_feats(jax.random.fold_in(key_of[17], 71), 0),
        "noise": scatter_about(key_of[1], (ITEMS_ALL, FRAMES, D), 0.1, 0.59765625, ((0, 8), (1, 4))),
        "starts": place_ends(jax.random.randint(key_of[2], (ITEMS_ALL, SPANS), 0, FRAMES), jax.random.fold_in(key_of[2], 1), 0, FRAMES - 1).astype(jnp.int32),
        "span_length": draw_span_length(jax.random.fold_in(key_of[17], 71), 0),
        "cotangent": bell_draw_with(key_of[4], (ITEMS_ALL, FRAMES, D), 1.0, 6.0, ((0, 8), (1, 4)), (0, 2, 8, 2.0)),
        "norm_gains": jnp.clip(1.0 + 0.18 * jax.random.normal(key_of[5], (NORMS, D), jnp.float32), 0.1, 1.9),
        "ffn1_in": scatter_about(key_of[6], (D, FF), D ** -0.5, 0.1875, ((0, 8), (1, 4))),
        "ffn1_out": scatter_about(key_of[7], (D, FF), FF ** -0.5, 0.09375, ((0, 8), (1, 4))),
        "qkv_weight": scatter_about(key_of[8], (D, 3, D), D ** -0.5, 0.1875, ((0, 8), (2, 4))),
        "attn_out": scatter_about(key_of[9], (D, D), (D // 64) ** -0.5, 1.5, ((0, 8), (1, 4))),
        "conv_in": scatter_about(key_of[10], (D, 2, D), D ** -0.5, 0.1875, ((0, 8), (2, 4))),
        "conv_kernel": scatter_about(key_of[11], (KERNEL, D), KERNEL ** -0.5, 2.5, (), jnp.float32),
        "batch_gain": jnp.clip(1.0 + 0.18 * jax.random.normal(key_of[12], (D,), jnp.float32), 0.1, 1.9),
        "batch_bias": scatter_about(key_of[13], (D,), 0.5, 3.0, ((0, 4),), jnp.float32),
        "conv_out": scatter_about(key_of[14], (D, D), D ** -0.5, 0.1875, ((0, 8), (1, 4))),
        "ffn2_in": scatter_about(key_of[15], (D, FF), D ** -0.5, 0.1875, ((0, 8), (1, 4))),
        "ffn2_out": scatter_about(key_of[16], (D, FF), FF ** -0.5, 0.09375, ((0, 8), (1, 4))),
    }


@jax.custom_vjp
def low(v):
    return lax.optimization_barrier(v.astype(jnp.bfloat16)).astype(jnp.float32)

@jax.custom_vjp
def low_back(v):
    return v

def low_keep(v):
    return (low(v), None)

def low_pass(kept, grad):
    return (grad,)

def back_keep(v):
    return (v, None)

def back_low(kept, grad):
    return (low(grad),)
low.defvjp(low_keep, low_pass)
low_back.defvjp(back_keep, back_low)
highest = lax.Precision.HIGHEST
eps_norm = 1e-05
eps_batch = 1e-05

def span_mask(starts, span_length):
    frames = jnp.arange(FRAMES, dtype=jnp.int32)
    finish = starts + span_length[:, None]
    inside = (frames[None, None, :] >= starts[:, :, None]) & (frames[None, None, :] < finish[:, :, None])
    return jnp.any(inside, axis=1)

def layer_norm(stream, norm_gain):
    centred = stream - lax.optimization_barrier(jnp.mean(stream, axis=-1, keepdims=True))
    spread = lax.optimization_barrier(jnp.mean(centred * centred, axis=-1, keepdims=True))
    return centred * lax.rsqrt(spread + eps_norm) * norm_gain

def swish(values):
    return values * jax.nn.sigmoid(values)

def feed_forward(stream, norm_gain, weight_in, weight_out):
    normed = low(layer_norm(stream, norm_gain))
    hidden = low_back(jnp.einsum('itd,df->itf', normed, weight_in, precision=highest))
    active = low(swish(hidden))
    output = low_back(jnp.einsum('itf,df->itd', active, weight_out, precision=highest))
    return stream + 0.5 * output

def attend_block(block):
    queries = block[:, :, 0]
    key_rows = block[:, :, 1]
    value_rows = block[:, :, 2]
    scores = low_back(jnp.einsum('iqhe,ikhe->ihqk', queries, key_rows, precision=highest) * HEAD_DIM ** (-0.5))
    probs = low(jax.nn.softmax(scores, axis=-1))
    return jnp.einsum('ihqk,ikhe->iqhe', probs, value_rows, precision=highest)

def attention(stream, norm_gain, weight_in, weight_out):
    normed = low(layer_norm(stream, norm_gain))
    project = low(low_back(jnp.einsum('itd,dch->itch', normed, weight_in, precision=highest)))
    blocks = project.reshape(N_DP, ITEMS, FRAMES, 3, HEADS, HEAD_DIM)
    mixed = lax.map(jax.checkpoint(attend_block), blocks)
    mixed = low(low_back(mixed.reshape(ITEMS_ALL, FRAMES, D)))
    output = low_back(jnp.einsum('ite,de->itd', mixed, weight_out, precision=highest))
    return stream + output

def convolve(stream, norm_gain, weight_in, kernel, batch_gain, batch_bias, weight_out):
    normed = low(layer_norm(stream, norm_gain))
    paired = low_back(jnp.einsum('itd,dgc->itgc', normed, weight_in, precision=highest))
    gated = paired[:, :, 0] * jax.nn.sigmoid(paired[:, :, 1])
    reach = KERNEL // 2
    padded = jnp.pad(gated, ((0, 0), (reach, reach), (0, 0)))
    depthwise = sum((kernel[offset] * padded[:, offset:offset + FRAMES] for offset in range(KERNEL)))
    average = lax.optimization_barrier(jnp.mean(depthwise, axis=(0, 1)))
    centred = depthwise - average
    variance = lax.optimization_barrier(jnp.mean(centred * centred, axis=(0, 1)))
    batched = centred * lax.rsqrt(variance + eps_batch) * batch_gain + batch_bias
    active = low(swish(batched))
    output = low_back(jnp.einsum('itc,dc->itd', active, weight_out, precision=highest))
    return stream + output

def layer(masked, noise_float, feats, norm_gains, ffn1_in, ffn1_out, qkv_weight, attn_out, conv_in, conv_kernel, batch_gain, batch_bias, conv_out, ffn2_in, ffn2_out):
    stream = jnp.where(masked[:, :, None], noise_float, feats)
    stream = feed_forward(stream, norm_gains[0], ffn1_in, ffn1_out)
    stream = attention(stream, norm_gains[1], qkv_weight, attn_out)
    stream = convolve(stream, norm_gains[2], conv_in, conv_kernel, batch_gain, batch_bias, conv_out)
    stream = feed_forward(stream, norm_gains[3], ffn2_in, ffn2_out)
    return layer_norm(stream, norm_gains[4])

def reference(feats, noise, starts, span_length, cotangent, norm_gains, ffn1_in, ffn1_out, qkv_weight, attn_out, conv_in, conv_kernel, batch_gain, batch_bias, conv_out, ffn2_in, ffn2_out):
    masked = span_mask(starts, span_length)
    noise_float = noise.astype(jnp.float32)
    params = (feats, norm_gains, ffn1_in, ffn1_out, qkv_weight, attn_out, conv_in, conv_kernel, batch_gain, batch_bias, conv_out, ffn2_in, ffn2_out)
    floats = tuple((tensor.astype(jnp.float32) for tensor in params))

    def forward(*inputs):
        return layer(masked, noise_float, *inputs)
    output, backward = jax.vjp(forward, *floats)
    masked_float = masked.astype(jnp.float32)
    count = jnp.sum(masked_float)
    seed_grad = cotangent.astype(jnp.float32) * masked_float[:, :, None] * jnp.sqrt(TOKENS / count)
    grads = backward(seed_grad)
    return (output, grads[0], count, grads[1], grads[2], grads[3], grads[4], grads[5], grads[6], grads[7], grads[8], grads[9], grads[10], grads[11], grads[12])
```

```python
import jax
import jax.numpy as jnp
from jax import lax
from jax.sharding import PartitionSpec as P

HEAD_DIM = 128
eps_norm = 1e-05
eps_batch = 1e-05
bf16 = jnp.bfloat16
f32 = jnp.float32


def mm(left, right, left_dim, right_dim):
    return lax.dot_general(
        left, right, (((left_dim,), (right_dim,)), ((), ())), preferred_element_type=f32
    )


def swap(value, axis, distance):
    pairs = [(index, index ^ distance) for index in range(lax.axis_size(axis))]
    return lax.ppermute(value, axis, pairs)


class Cube:
    def __init__(self, size):
        self.bits = size.bit_length() - 1
        middle = tuple(range(self.bits - 1, 0, -1))
        self.first = middle + (0,)
        self.second = middle[::-1] + (0,)
        self.order = sorted(range(size), key=self.key)

    def key(self, label):
        return sum(((label >> bit) & 1) << place for place, bit in enumerate(self.first))

    def runs(self, entries):
        joined = []
        for source, place in entries:
            if joined and joined[-1][0] == source and joined[-1][2] == place:
                joined[-1][2] = place + 1
            else:
                joined.append([source, place, place + 1])
        return joined

    def rows(self, sources, entries, height):
        parts = [
            lax.slice_in_dim(sources[source], low * height, high * height, axis=0)
            for source, low, high in self.runs(entries)
        ]
        return parts[0] if len(parts) == 1 else jnp.concatenate(parts, axis=0)

    def gather(self, shard, order):
        height = shard.shape[0]
        held, labels = shard, [0]
        for bit in order[:-1]:
            taken = swap(held, "dp", 1 << bit)
            entries = [(label, 0, place) for place, label in enumerate(labels)]
            entries += [(label ^ (1 << bit), 1, place) for place, label in enumerate(labels)]
            entries.sort(key=lambda entry: self.key(entry[0]))
            held = self.rows((held, taken), [entry[1:] for entry in entries], height)
            labels = [entry[0] for entry in entries]
        return held, swap(held, "dp", 1)

    def scatter(self, low, high, order):
        labels = [label for label in self.order if not label & 1]
        height = low.shape[0] // len(labels)
        held = low.astype(f32) + swap(high.astype(bf16), "dp", 1).astype(f32)
        for bit in order[-2::-1]:
            held = held.astype(bf16)
            send = [(0, place) for place, label in enumerate(labels) if label >> bit & 1]
            keep = [(0, place) for place, label in enumerate(labels) if not label >> bit & 1]
            taken = swap(self.rows((held,), send, height), "dp", 1 << bit)
            held = self.rows((held,), keep, height).astype(f32) + taken.astype(f32)
            labels = [label for label in labels if not label >> bit & 1]
        return held


def halves(value):
    middle = value.shape[-1] // 2
    return value[..., :middle], value[..., middle:]


def span_mask(starts, span_length, length):
    frames = jnp.arange(length, dtype=jnp.int32)
    finish = starts + span_length[:, None]
    inside = (frames[None, None, :] >= starts[:, :, None]) & (
        frames[None, None, :] < finish[:, :, None]
    )
    return jnp.any(inside, axis=1)


def normalize(stream, norm_gain):
    centred = stream - jnp.mean(stream, axis=-1, keepdims=True)
    inverse = lax.rsqrt(jnp.mean(centred * centred, axis=-1, keepdims=True) + eps_norm)
    scaled = centred * inverse
    return (scaled * norm_gain, scaled, inverse)


def normalize_back(grad_normed, scaled, inverse, norm_gain):
    grad_scaled = grad_normed * norm_gain
    grad_gain = jnp.sum(grad_normed * scaled, axis=0)
    centre_term = jnp.mean(grad_scaled, axis=-1, keepdims=True)
    slope_term = jnp.mean(grad_scaled * scaled, axis=-1, keepdims=True)
    return (inverse * (grad_scaled - centre_term - scaled * slope_term), grad_gain)


def swish_slope(values):
    logistic = jax.nn.sigmoid(values)
    return logistic + values * logistic * (1.0 - logistic)


def join_pair(partial_value):
    mine = partial_value.astype(bf16)
    return mine.astype(f32) + swap(mine, "tp", 1).astype(f32)


def project_in(normed, weight):
    return sum(mm(part, rows, 1, 0) for part, rows in zip(halves(normed), weight))


def project_out(active, weight):
    return jnp.concatenate([mm(active, rows, 1, 1) for rows in weight], axis=1)


def outer(rows_side, columns_side):
    return [mm(part, columns_side, 0, 0).astype(bf16) for part in halves(rows_side)]


def ffn_forward(stream, norm_gain, groups):
    normed, scaled, inverse = normalize(stream, norm_gain)
    whole_in = normed.astype(bf16)
    saved, partial_value = [], 0.0
    for weight_in, weight_out in groups:
        hidden = project_in(whole_in, weight_in)
        active = (hidden * jax.nn.sigmoid(hidden)).astype(bf16)
        partial_value = partial_value + project_out(active, weight_out)
        saved.append((hidden, active))
    return stream + 0.5 * join_pair(partial_value), (scaled, inverse, whole_in, saved)


def ffn_backward(grad_stream, saved, norm_gain, groups):
    scaled, inverse, whole_in, states = saved
    whole_grad = (0.5 * grad_stream).astype(bf16)
    grads, partial_value = [], 0.0
    for (weight_in, weight_out), (hidden, active) in zip(groups, states):
        grad_active = project_in(whole_grad, weight_out)
        grad_hidden = (grad_active * swish_slope(hidden)).astype(bf16)
        partial_value = partial_value + project_out(grad_hidden, weight_in)
        grads.append((outer(whole_in, grad_hidden), outer(whole_grad, active)))
    grad_normed = join_pair(partial_value)
    grad_local, grad_gain = normalize_back(grad_normed, scaled, inverse, norm_gain)
    return grad_stream + grad_local, grad_gain, grads


def split_heads(project):
    quarter = project.shape[1] // 2
    width = quarter // 3
    pieces = []
    for kind in range(3):
        columns = [
            base + kind * width + head
            for base in (0, quarter)
            for head in range(0, width, HEAD_DIM)
        ]
        pieces.append(jnp.stack([project[:, at : at + HEAD_DIM] for at in columns]))
    return pieces


def merge_heads(pieces):
    heads = pieces[0].shape[0] // 2
    return jnp.concatenate(
        [
            piece[base + head]
            for base in (0, heads)
            for piece in pieces
            for head in range(heads)
        ],
        axis=1,
    )


def attn_forward(stream, norm_gain, weight_in, weight_out):
    normed, scaled, inverse = normalize(stream, norm_gain)
    whole_in = normed.astype(bf16)
    project = project_in(whole_in, weight_in).astype(bf16)
    queries, key_rows, value_rows = split_heads(project)
    scores = jnp.einsum(
        "hqe,hke->hqk", queries, key_rows, preferred_element_type=f32
    ) * HEAD_DIM ** (-0.5)
    highest = jnp.max(scores, axis=-1, keepdims=True)
    raised = jnp.exp(scores - highest)
    probs = raised / jnp.sum(raised, axis=-1, keepdims=True)
    mixed = jnp.einsum(
        "hqk,hke->hqe", probs.astype(bf16), value_rows, preferred_element_type=f32
    ).astype(bf16)
    mixed = jnp.concatenate([mixed[head] for head in range(mixed.shape[0])], axis=1)
    partial_value = project_out(mixed, weight_out)
    saved = (scaled, inverse, whole_in, queries, key_rows, value_rows, probs, mixed)
    return stream + join_pair(partial_value), saved


def attn_backward(grad_stream, saved, norm_gain, weight_in, weight_out):
    scaled, inverse, whole_in, queries, key_rows, value_rows, probs, mixed = saved
    whole_grad = grad_stream.astype(bf16)
    grad_second = outer(whole_grad, mixed)
    grad_mixed = project_in(whole_grad, weight_out).astype(bf16)
    heads = queries.shape[0]
    grad_mixed = jnp.stack(
        [grad_mixed[:, head * HEAD_DIM : (head + 1) * HEAD_DIM] for head in range(heads)]
    )
    factor = HEAD_DIM ** (-0.5)
    grad_values = jnp.einsum(
        "hqk,hqe->hke", probs.astype(bf16), grad_mixed, preferred_element_type=f32
    )
    grad_probs = jnp.einsum("hqe,hke->hqk", grad_mixed, value_rows, preferred_element_type=f32)
    grad_scores = (
        probs * (grad_probs - jnp.sum(probs * grad_probs, axis=-1, keepdims=True))
    ).astype(bf16)
    grad_queries = (
        jnp.einsum("hqk,hke->hqe", grad_scores, key_rows, preferred_element_type=f32) * factor
    )
    grad_keys = (
        jnp.einsum("hqk,hqe->hke", grad_scores, queries, preferred_element_type=f32) * factor
    )
    grad_project = merge_heads(
        [part.astype(bf16) for part in (grad_queries, grad_keys, grad_values)]
    )
    grad_first = outer(whole_in, grad_project)
    grad_normed = join_pair(project_out(grad_project, weight_in))
    grad_local, grad_gain = normalize_back(grad_normed, scaled, inverse, norm_gain)
    return grad_stream + grad_local, grad_gain, grad_first, grad_second


def sum_items(rows):
    for bit in range(lax.axis_size("dp").bit_length() - 1):
        rows = rows + swap(rows, "dp", 1 << bit)
    other = swap(rows, "tp", 2)
    first, second = halves(other)
    return rows + jnp.concatenate([second, first], axis=-1)


def shifted(value, amount):
    frames = value.shape[0]
    if amount == 0:
        return value
    edge = jnp.zeros((abs(amount), value.shape[1]), value.dtype)
    if amount > 0:
        return jnp.concatenate([value[amount:], edge], axis=0)
    return jnp.concatenate([edge, value[: frames + amount]], axis=0)


def value_gate(paired):
    quarter = paired.shape[1] // 2
    width = quarter // 2
    return [
        jnp.concatenate(
            [paired[:, at : at + width] for at in (kind * width, quarter + kind * width)], axis=1
        )
        for kind in (0, 1)
    ]


def conv_forward(
    stream, norm_gain, weight_in, kernel_local, batch_gain, batch_bias, weight_out, masked_own, population
):
    normed, scaled, inverse = normalize(stream, norm_gain)
    whole_in = normed.astype(bf16)
    paired = project_in(whole_in, weight_in)
    values_part, gate = value_gate(paired)
    gated = values_part * jax.nn.sigmoid(gate)
    taps = kernel_local.shape[0]
    reach = taps // 2
    depthwise = sum(
        kernel_local[offset] * shifted(gated, offset - reach) for offset in range(taps)
    )
    sums = jnp.stack(
        [
            jnp.sum(depthwise, axis=0),
            jnp.sum(depthwise * depthwise, axis=0),
            jnp.broadcast_to(masked_own, depthwise.shape[1:]),
        ]
    )
    sums = sum_items(sums)
    average = sums[0] / population
    variance = sums[1] / population - average * average
    batch_inverse = lax.rsqrt(variance + eps_batch)
    normal = (depthwise - average) * batch_inverse
    batched = normal * batch_gain + batch_bias
    active = (batched * jax.nn.sigmoid(batched)).astype(bf16)
    partial_value = project_out(active, weight_out)
    saved = (
        scaled, inverse, whole_in, values_part, gate, gated, normal, batch_inverse, batched, active
    )
    return stream + join_pair(partial_value), saved, sums[2, 0]


def conv_backward(
    grad_stream, saved, norm_gain, weight_in, kernel_local, batch_gain, weight_out, population
):
    scaled, inverse, whole_in, values_part, gate, gated, normal, batch_inverse, batched, active = saved
    whole_grad = grad_stream.astype(bf16)
    grad_active = project_in(whole_grad, weight_out)
    grad_batched = grad_active * swish_slope(batched)
    grad_bias, grad_scale = sum_items(
        jnp.stack([jnp.sum(grad_batched, axis=0), jnp.sum(grad_batched * normal, axis=0)])
    )
    grad_second = outer(whole_grad, active)
    grad_depth = (
        batch_inverse
        * batch_gain
        * (grad_batched - grad_bias / population - normal * (grad_scale / population))
    )
    taps = kernel_local.shape[0]
    reach = taps // 2
    grad_kernel = jnp.stack(
        [jnp.sum(grad_depth * shifted(gated, offset - reach), axis=0) for offset in range(taps)]
    )
    grad_gated = sum(
        kernel_local[offset] * shifted(grad_depth, reach - offset) for offset in range(taps)
    )
    logistic = jax.nn.sigmoid(gate)
    first, second = halves((grad_gated * logistic).astype(bf16))
    third, fourth = halves((grad_gated * values_part * logistic * (1.0 - logistic)).astype(bf16))
    grad_paired = jnp.concatenate([first, third, second, fourth], axis=1)
    grad_first = outer(whole_in, grad_paired)
    grad_normed = join_pair(project_out(grad_paired, weight_in))
    grad_local, grad_gain = normalize_back(grad_normed, scaled, inverse, norm_gain)
    return (
        grad_stream + grad_local,
        grad_gain,
        grad_first,
        grad_second,
        grad_kernel,
        grad_scale,
        grad_bias,
    )


def pick(value, index):
    return lax.dynamic_index_in_dim(value, index, 0, keepdims=False)


def on_device(
    feats,
    noise,
    starts,
    span_length,
    cotangent,
    norm_gains,
    ffn1_in,
    ffn1_out,
    qkv_weight,
    attn_out,
    conv_in,
    conv_kernel,
    batch_gain,
    batch_bias,
    conv_out,
    ffn2_in,
    ffn2_out,
):
    local_frames, width = feats.shape[1], feats.shape[2]
    parts = lax.axis_size("tp")
    replicas = lax.axis_size("dp")
    assert parts == 4 and feats.shape[0] == 2
    whole_frames = local_frames * parts
    population = whole_frames * feats.shape[0] * replicas
    place = lax.axis_index("tp")
    item = place // 2
    channels = batch_gain.shape[0]
    cube = Cube(replicas)
    block = width // replicas

    columns = jnp.arange(width, dtype=jnp.int32)
    position = sum(
        jnp.where(columns // block == at, label, 0) for at, label in enumerate(cube.order)
    )
    source = (position ^ lax.axis_index("dp")) * block + columns % block
    moved = columns[:, None] == source[None, :]

    def to_stream(rows):
        return mm(rows, moved.astype(rows.dtype), 1, 0)

    def exact(rows, contract):
        return lax.dot_general(
            rows,
            moved.astype(f32),
            (((1,), (contract,)), ((), ())),
            precision=lax.Precision.HIGHEST,
        )

    masked = span_mask(starts, span_length, whole_frames)
    local_mask = lax.dynamic_slice_in_dim(masked, place * local_frames, local_frames, 1)[:, :, None]
    entered = jnp.stack(
        [jnp.where(local_mask, noise, feats), jnp.where(local_mask, cotangent, jnp.zeros((), bf16))],
        axis=1,
    )

    first_shard = jnp.concatenate([ffn1_in, ffn1_out], axis=1)
    first_other = swap(first_shard, "tp", 2)
    own = pick(entered, item)
    near = jnp.stack([own, swap(pick(entered, 1 - item), "tp", 2)])
    far = swap(near, "tp", 1)
    relative = jnp.stack([near[0], far[0], near[1], far[1]])
    ordered = jnp.stack([pick(relative, place ^ chunk) for chunk in range(parts)])
    ordered = ordered.transpose(1, 0, 2, 3).reshape(2 * whole_frames, width)
    ordered = to_stream(ordered)
    stream, seed = ordered[:whole_frames], ordered[whole_frames:]
    gains = exact(norm_gains, 0)

    hidden_width = ffn1_in.shape[1]
    first_groups = [
        (cube.gather(ffn1_in, cube.first), cube.gather(ffn1_out, cube.second)),
        (
            cube.gather(first_other[:, :hidden_width], cube.first),
            cube.gather(first_other[:, hidden_width:], cube.second),
        ),
    ]
    rows = ffn1_in.shape[0]
    rest = [
        qkv_weight.reshape(rows, -1), attn_out, conv_in.reshape(rows, -1), conv_out, ffn2_in, ffn2_out
    ]
    joined = swap(jnp.concatenate(rest, axis=1), "tp", 2)
    doubled, at = [], 0
    for shard in rest:
        doubled.append(
            jnp.concatenate([shard, joined[:, at : at + shard.shape[1]]], axis=1)
        )
        at += shard.shape[1]
    attn_weights = cube.gather(doubled[0], cube.first), cube.gather(doubled[1], cube.second)
    conv_weights = cube.gather(doubled[2], cube.second), cube.gather(doubled[3], cube.first)
    second_groups = [(cube.gather(doubled[4], cube.first), cube.gather(doubled[5], cube.second))]

    batch_pair = jnp.stack([batch_gain, batch_bias])
    batch_gain, batch_bias = jnp.concatenate([batch_pair, swap(batch_pair, "tp", 2)], axis=1)
    kernel_local = jnp.concatenate(
        [
            lax.dynamic_slice_in_dim(conv_kernel, start * channels, channels, 1)
            for start in (place, place ^ 2)
        ],
        axis=1,
    )

    stream, first_saved = ffn_forward(stream, gains[0], first_groups)
    stream, attn_saved = attn_forward(stream, gains[1], *attn_weights)
    masked_own = jnp.sum(pick(masked, item).astype(f32))
    stream, conv_saved, masked_total = conv_forward(
        stream,
        gains[2],
        conv_weights[0],
        kernel_local,
        batch_gain,
        batch_bias,
        conv_weights[1],
        masked_own,
        population,
    )
    stream, second_saved = ffn_forward(stream, gains[3], second_groups)
    final_out, final_scaled, final_inverse = normalize(stream, gains[4])

    def deliver(value):
        chunks = value.astype(bf16).reshape(parts, local_frames, width)
        both = jnp.concatenate([pick(chunks, place), pick(chunks, place ^ 2)], axis=0)
        both = mm(both, moved.astype(bf16), 1, 1)
        mine = both[:local_frames]
        other = swap(both[local_frames:].astype(bf16), "tp", 2).astype(f32)
        return jnp.stack(
            [jnp.where(item == 0, mine, other), jnp.where(item == 0, other, mine)]
        )

    layer_out = deliver(final_out)
    grad_stream, gain_final = normalize_back(
        seed * jnp.sqrt(population / masked_total), final_scaled, final_inverse, gains[4]
    )

    def settle(low_high, order):
        return cube.scatter(*low_high, order)

    def settle_pair(held):
        mine, other = halves(held)
        return mine + swap(other.astype(bf16), "tp", 2).astype(f32)

    grad_stream, gain_second, second_grads = ffn_backward(
        grad_stream, second_saved, gains[3], second_groups
    )
    second_in_grad = settle_pair(settle(second_grads[0][0], cube.first))
    second_out_grad = settle_pair(settle(second_grads[0][1], cube.second))
    grad_stream, gain_conv, grad_first, grad_second, kernel_part, grad_scale, grad_bias = conv_backward(
        grad_stream,
        conv_saved,
        gains[2],
        conv_weights[0],
        kernel_local,
        batch_gain,
        conv_weights[1],
        population,
    )
    conv_in_grad = settle_pair(settle(grad_first, cube.second)).reshape(conv_in.shape)
    conv_out_grad = settle_pair(settle(grad_second, cube.first))
    grad_stream, gain_attn, grad_first, grad_second = attn_backward(
        grad_stream, attn_saved, gains[1], *attn_weights
    )
    qkv_grad = settle_pair(settle(grad_first, cube.first)).reshape(qkv_weight.shape)
    attn_out_grad = settle_pair(settle(grad_second, cube.second))
    grad_stream, gain_first, first_grads = ffn_backward(
        grad_stream, first_saved, gains[0], first_groups
    )
    other_in = settle(first_grads[1][0], cube.first)
    other_out = settle(first_grads[1][1], cube.second)
    other = swap(jnp.concatenate([other_in, other_out], axis=1).astype(bf16), "tp", 2).astype(f32)
    first_in_grad = settle(first_grads[0][0], cube.first) + other[:, :hidden_width]
    first_out_grad = settle(first_grads[0][1], cube.second) + other[:, hidden_width:]

    gain_grads = jnp.stack((gain_first, gain_attn, gain_conv, gain_second, gain_final))
    gain_grads = 0.5 * exact(gain_grads, 1)
    kernel_full = jnp.zeros(conv_kernel.shape, f32)
    for quarter, start in enumerate((place, place ^ 2)):
        kernel_full = lax.dynamic_update_slice_in_dim(
            kernel_full,
            kernel_part[:, quarter * channels : (quarter + 1) * channels],
            start * channels,
            1,
        )
    small = jnp.concatenate([gain_grads, kernel_full], axis=0)
    for bit in range(cube.bits):
        small = small + swap(small, "dp", 1 << bit)
    small = small + swap(small, "tp", 2)
    small = small + swap(small, "tp", 1)
    norms = norm_gains.shape[0]
    mask_own = pick(masked, item)[:, None]
    feats_grad = deliver(jnp.where(mask_own, 0.0, grad_stream))
    return (
        layer_out,
        feats_grad,
        masked_total,
        small[:norms],
        first_in_grad,
        first_out_grad,
        qkv_grad,
        attn_out_grad,
        conv_in_grad,
        small[norms:],
        grad_scale[:channels],
        grad_bias[:channels],
        conv_out_grad,
        second_in_grad,
        second_out_grad,
    )


def solution(mesh):
    return jax.shard_map(
        on_device,
        mesh=mesh,
        in_specs=(
            P("dp", "tp", None),
            P("dp", "tp", None),
            P("dp", None),
            P("dp"),
            P("dp", "tp", None),
            P(),
            P("dp", "tp"),
            P("dp", "tp"),
            P("dp", None, "tp"),
            P("dp", "tp"),
            P("dp", None, "tp"),
            P(),
            P("tp"),
            P("tp"),
            P("dp", "tp"),
            P("dp", "tp"),
            P("dp", "tp"),
        ),
        out_specs=(
            P("dp", "tp", None),
            P("dp", "tp", None),
            P(),
            P(),
            P("dp", "tp"),
            P("dp", "tp"),
            P("dp", None, "tp"),
            P("dp", "tp"),
            P("dp", None, "tp"),
            P(),
            P("tp"),
            P("tp"),
            P("dp", "tp"),
            P("dp", "tp"),
            P("dp", "tp"),
        ),
        check_vma=False,
    )
```

```python
import jax
import jax.numpy as jnp
from jax import lax
from jax.sharding import PartitionSpec as P

HEAD_DIM = 128
eps_norm = 1e-05
eps_batch = 1e-05
bf16 = jnp.bfloat16
f32 = jnp.float32


def mm(left, right, left_dim, right_dim):
    return lax.dot_general(
        left, right, (((left_dim,), (right_dim,)), ((), ())), preferred_element_type=f32
    )


def swap(value, axis, distance):
    pairs = [(index, index ^ distance) for index in range(lax.axis_size(axis))]
    return lax.ppermute(value, axis, pairs)


class Cube:
    def __init__(self, size):
        self.bits = size.bit_length() - 1
        middle = tuple(range(self.bits - 1, 0, -1))
        self.first = middle + (0,)
        self.second = middle[::-1] + (0,)
        self.order = sorted(range(size), key=self.key)

    def key(self, label):
        return sum(((label >> bit) & 1) << place for place, bit in enumerate(self.first))

    def runs(self, entries):
        joined = []
        for source, place in entries:
            if joined and joined[-1][0] == source and joined[-1][2] == place:
                joined[-1][2] = place + 1
            else:
                joined.append([source, place, place + 1])
        return joined

    def rows(self, sources, entries, height):
        parts = [
            lax.slice_in_dim(sources[source], low * height, high * height, axis=0)
            for source, low, high in self.runs(entries)
        ]
        return parts[0] if len(parts) == 1 else jnp.concatenate(parts, axis=0)

    def gather(self, shard, order):
        height = shard.shape[0]
        held, labels = shard, [0]
        for bit in order[:-1]:
            taken = yield held, "dp", 1 << bit
            entries = [(label, 0, place) for place, label in enumerate(labels)]
            entries += [(label ^ (1 << bit), 1, place) for place, label in enumerate(labels)]
            entries.sort(key=lambda entry: self.key(entry[0]))
            held = self.rows((held, taken), [entry[1:] for entry in entries], height)
            labels = [entry[0] for entry in entries]
        taken = yield held, "dp", 1
        return held, taken

    def scatter(self, low, high, order):
        labels = [label for label in self.order if not label & 1]
        height = low.shape[0] // len(labels)
        taken = yield high, "dp", 1
        held = low.astype(f32) + taken.astype(f32)
        for bit in order[-2::-1]:
            held = held.astype(bf16)
            send = [(0, place) for place, label in enumerate(labels) if label >> bit & 1]
            keep = [(0, place) for place, label in enumerate(labels) if not label >> bit & 1]
            taken = yield self.rows((held,), send, height), "dp", 1 << bit
            held = self.rows((held,), keep, height).astype(f32) + taken.astype(f32)
            labels = [label for label in labels if not label >> bit & 1]
        return held


class Move:
    def __init__(self, steps, left=1):
        self.steps, self.left, self.result = steps, left, None
        self.request = next(steps)

    def advance(self, taken):
        self.left -= 1
        try:
            self.request = self.steps.send(taken)
        except StopIteration as end:
            self.request, self.result = None, end.value


def once(value, axis, distance):
    taken = yield value, axis, distance
    return taken


def tie(*values):
    return lax.optimization_barrier(values)


def issue(anchor, *moves):
    *values, anchor = tie(*[move.request[0] for move in moves], anchor)
    for move, value in zip(moves, values):
        move.flying = swap(value, *move.request[1:])
    return anchor


def wait(anchor, *moves):
    *values, anchor = tie(*[move.flying for move in moves], anchor)
    for move, value in zip(moves, values):
        move.advance(value)
    return anchor


def fly(anchor, left, *moves):
    while moves[0].left > left:
        anchor = wait(issue(anchor, *moves), *moves)
    return issue(anchor, *moves)


def halves(value):
    middle = value.shape[-1] // 2
    return value[..., :middle], value[..., middle:]


def span_mask(starts, span_length, length):
    frames = jnp.arange(length, dtype=jnp.int32)
    finish = starts + span_length[:, None]
    inside = (frames[None, None, :] >= starts[:, :, None]) & (
        frames[None, None, :] < finish[:, :, None]
    )
    return jnp.any(inside, axis=1)


def normalize(stream, norm_gain):
    centred = stream - jnp.mean(stream, axis=-1, keepdims=True)
    inverse = lax.rsqrt(jnp.mean(centred * centred, axis=-1, keepdims=True) + eps_norm)
    scaled = centred * inverse
    return (scaled * norm_gain, scaled, inverse)


def normalize_back(grad_normed, scaled, inverse, norm_gain):
    grad_scaled = grad_normed * norm_gain
    grad_gain = jnp.sum(grad_normed * scaled, axis=0)
    centre_term = jnp.mean(grad_scaled, axis=-1, keepdims=True)
    slope_term = jnp.mean(grad_scaled * scaled, axis=-1, keepdims=True)
    return (inverse * (grad_scaled - centre_term - scaled * slope_term), grad_gain)


def swish_slope(values):
    logistic = jax.nn.sigmoid(values)
    return logistic + values * logistic * (1.0 - logistic)


def pair_sum(partial_value):
    mine = partial_value.astype(bf16)
    taken = yield mine, "tp", 1
    return mine.astype(f32) + taken.astype(f32)


def project_in(normed, weight):
    return sum(mm(part, rows, 1, 0) for part, rows in zip(halves(normed), weight))


def project_out(active, weight):
    return jnp.concatenate([mm(active, rows, 1, 1) for rows in weight], axis=1)


def outer(rows_side, columns_side):
    return [mm(part, columns_side, 0, 0).astype(bf16) for part in halves(rows_side)]


def ffn_forward(whole_in, weight_in, weight_out):
    hidden = project_in(whole_in, weight_in)
    active = (hidden * jax.nn.sigmoid(hidden)).astype(bf16)
    return project_out(active, weight_out), (hidden, active)


def ffn_backward(whole_grad, state, weight_in, weight_out):
    grad_active = project_in(whole_grad, weight_out)
    grad_hidden = (grad_active * swish_slope(state[0])).astype(bf16)
    return project_out(grad_hidden, weight_in), grad_hidden


def split_heads(project):
    quarter = project.shape[1] // 2
    width = quarter // 3
    pieces = []
    for kind in range(3):
        columns = [
            base + kind * width + head
            for base in (0, quarter)
            for head in range(0, width, HEAD_DIM)
        ]
        pieces.append(jnp.stack([project[:, at : at + HEAD_DIM] for at in columns]))
    return pieces


def merge_heads(pieces):
    heads = pieces[0].shape[0] // 2
    return jnp.concatenate(
        [
            piece[base + head]
            for base in (0, heads)
            for piece in pieces
            for head in range(heads)
        ],
        axis=1,
    )


def attn_forward(whole_in, weight_in):
    project = project_in(whole_in, weight_in).astype(bf16)
    queries, key_rows, value_rows = split_heads(project)
    scores = jnp.einsum(
        "hqe,hke->hqk", queries, key_rows, preferred_element_type=f32
    ) * HEAD_DIM ** (-0.5)
    highest = jnp.max(scores, axis=-1, keepdims=True)
    raised = jnp.exp(scores - highest)
    probs = raised / jnp.sum(raised, axis=-1, keepdims=True)
    mixed = jnp.einsum(
        "hqk,hke->hqe", probs.astype(bf16), value_rows, preferred_element_type=f32
    ).astype(bf16)
    mixed = jnp.concatenate([mixed[head] for head in range(mixed.shape[0])], axis=1)
    return mixed, (queries, key_rows, value_rows, probs)


def attn_backward(whole_grad, saved, weight_out):
    queries, key_rows, value_rows, probs = saved
    grad_mixed = project_in(whole_grad, weight_out).astype(bf16)
    heads = queries.shape[0]
    grad_mixed = jnp.stack(
        [grad_mixed[:, head * HEAD_DIM : (head + 1) * HEAD_DIM] for head in range(heads)]
    )
    factor = HEAD_DIM ** (-0.5)
    grad_values = jnp.einsum(
        "hqk,hqe->hke", probs.astype(bf16), grad_mixed, preferred_element_type=f32
    )
    grad_probs = jnp.einsum("hqe,hke->hqk", grad_mixed, value_rows, preferred_element_type=f32)
    grad_scores = (
        probs * (grad_probs - jnp.sum(probs * grad_probs, axis=-1, keepdims=True))
    ).astype(bf16)
    grad_queries = (
        jnp.einsum("hqk,hke->hqe", grad_scores, key_rows, preferred_element_type=f32) * factor
    )
    grad_keys = (
        jnp.einsum("hqk,hqe->hke", grad_scores, queries, preferred_element_type=f32) * factor
    )
    return merge_heads([part.astype(bf16) for part in (grad_queries, grad_keys, grad_values)])


def sum_items(rows):
    for bit in range(lax.axis_size("dp").bit_length() - 1):
        rows = rows + swap(rows, "dp", 1 << bit)
    other = swap(rows, "tp", 2)
    first, second = halves(other)
    return rows + jnp.concatenate([second, first], axis=-1)


def shifted(value, amount):
    frames = value.shape[0]
    if amount == 0:
        return value
    edge = jnp.zeros((abs(amount), value.shape[1]), value.dtype)
    if amount > 0:
        return jnp.concatenate([value[amount:], edge], axis=0)
    return jnp.concatenate([edge, value[: frames + amount]], axis=0)


def value_gate(paired):
    quarter = paired.shape[1] // 2
    width = quarter // 2
    return [
        jnp.concatenate(
            [paired[:, at : at + width] for at in (kind * width, quarter + kind * width)], axis=1
        )
        for kind in (0, 1)
    ]


def depth_mix(kernel_local, value, sign):
    reach = kernel_local.shape[0] // 2
    return sum(
        kernel_local[offset] * shifted(value, sign * (offset - reach))
        for offset in range(kernel_local.shape[0])
    )


def conv_backward(grad_batched, sums, saved, kernel_local, batch_gain, population):
    values_part, gate, gated, normal, batch_inverse = saved
    grad_bias, grad_scale = sums
    grad_depth = (
        batch_inverse
        * batch_gain
        * (grad_batched - grad_bias / population - normal * (grad_scale / population))
    )
    taps = kernel_local.shape[0]
    grad_kernel = jnp.stack(
        [jnp.sum(grad_depth * shifted(gated, tap - taps // 2), axis=0) for tap in range(taps)]
    )
    grad_gated = depth_mix(kernel_local, grad_depth, -1)
    logistic = jax.nn.sigmoid(gate)
    first, second = halves((grad_gated * logistic).astype(bf16))
    third, fourth = halves((grad_gated * values_part * logistic * (1.0 - logistic)).astype(bf16))
    return jnp.concatenate([first, third, second, fourth], axis=1), grad_kernel


def pick(value, index):
    return lax.dynamic_index_in_dim(value, index, 0, keepdims=False)


def on_device(
    feats,
    noise,
    starts,
    span_length,
    cotangent,
    norm_gains,
    ffn1_in,
    ffn1_out,
    qkv_weight,
    attn_out,
    conv_in,
    conv_kernel,
    batch_gain,
    batch_bias,
    conv_out,
    ffn2_in,
    ffn2_out,
):
    local_frames, width = feats.shape[1], feats.shape[2]
    parts = lax.axis_size("tp")
    replicas = lax.axis_size("dp")
    assert parts == 4 and feats.shape[0] == 2
    whole_frames = local_frames * parts
    population = whole_frames * feats.shape[0] * replicas
    place = lax.axis_index("tp")
    item = place // 2
    channels = batch_gain.shape[0]
    cube = Cube(replicas)
    block = width // replicas

    columns = jnp.arange(width, dtype=jnp.int32)
    position = sum(
        jnp.where(columns // block == at, label, 0) for at, label in enumerate(cube.order)
    )
    source = (position ^ lax.axis_index("dp")) * block + columns % block
    moved = columns[:, None] == source[None, :]

    def to_stream(rows):
        return mm(rows, moved.astype(rows.dtype), 1, 0)

    def exact(rows, contract):
        return lax.dot_general(
            rows,
            moved.astype(f32),
            (((1,), (contract,)), ((), ())),
            precision=lax.Precision.HIGHEST,
        )

    steps = cube.bits

    def gathering(shard, order):
        return Move(cube.gather(shard, order), steps)

    def scattering(low_high, order):
        return Move(cube.scatter(*low_high, order), steps)

    def across(value):
        return Move(once(value, "tp", 2))

    masked = span_mask(starts, span_length, whole_frames)
    local_mask = lax.dynamic_slice_in_dim(masked, place * local_frames, local_frames, 1)[:, :, None]
    entered = jnp.where(local_mask, noise, feats)
    pulled = jnp.where(local_mask, cotangent, jnp.zeros((), bf16))
    rows, hidden_width = ffn1_in.shape

    def whole_item(own, other):
        relative = jnp.stack([own[0], other[0], own[1], other[1]])
        ordered = jnp.stack([pick(relative, place ^ chunk) for chunk in range(parts)])
        return to_stream(ordered.reshape(whole_frames, width))

    anchor = span_length
    first_own = gathering(ffn1_in, cube.first), gathering(ffn1_out, cube.second)
    first_swap = across(ffn1_in), across(ffn1_out)
    item_swap = across(pick(entered, 1 - item))
    anchor = issue(anchor, *first_own, first_swap[0], item_swap)
    anchor = wait(anchor, *first_own, first_swap[0], item_swap)
    anchor = fly(anchor, 2, *first_own)
    anchor = issue(anchor, first_swap[1])
    anchor = wait(anchor, *first_own, first_swap[1])
    near = jnp.stack([pick(entered, item), item_swap.result])
    far = Move(once(near, "tp", 1))
    first_other = (
        gathering(first_swap[0].result, cube.first),
        gathering(first_swap[1].result, cube.second),
    )
    anchor = issue(anchor, *first_own, *first_other, far)
    anchor = wait(anchor, *first_own, *first_other, far)
    attn_shard = jnp.concatenate([qkv_weight.reshape(rows, -1), attn_out], axis=1)
    attn_swap = across(attn_shard)
    anchor = fly(anchor, 2, *first_other)
    anchor = issue(anchor, attn_swap)
    stream = whole_item(near, far.result)
    gains = exact(norm_gains, 0)
    normed, first_scaled, first_inverse = normalize(stream, gains[0])
    first_input = normed.astype(bf16)
    first_weights = [[move.result for move in first_own]]
    partial_own, state = ffn_forward(first_input, *first_weights[0])
    first_states = [state]
    anchor = wait(anchor, *first_other)
    anchor = wait(anchor, attn_swap)

    def doubled(shard, other):
        return jnp.concatenate([shard, other], axis=1)

    qkv_width = 3 * qkv_weight.shape[2]
    attn_moves = (
        gathering(
            doubled(attn_shard[:, :qkv_width], attn_swap.result[:, :qkv_width]), cube.first
        ),
        gathering(
            doubled(attn_shard[:, qkv_width:], attn_swap.result[:, qkv_width:]), cube.second
        ),
    )
    anchor = issue(anchor, *first_other, *attn_moves)
    anchor = wait(anchor, *first_other)
    conv_shard = jnp.concatenate([conv_in.reshape(rows, -1), conv_out], axis=1)
    conv_swap, pulled_swap = across(conv_shard), across(pick(pulled, 1 - item))
    anchor = issue(anchor, conv_swap, pulled_swap)
    first_weights.append([move.result for move in first_other])
    partial_value, state = ffn_forward(first_input, *first_weights[1])
    first_states.append(state)
    pair = Move(pair_sum(partial_own + partial_value))
    anchor = wait(anchor, *attn_moves)
    anchor = fly(anchor, 2, *attn_moves)
    anchor = issue(anchor, pair)
    anchor = wait(anchor, pair)
    stream = stream + 0.5 * pair.result

    normed, attn_scaled, attn_inverse = normalize(stream, gains[1])
    attn_input = normed.astype(bf16)
    anchor = wait(anchor, *attn_moves, conv_swap, pulled_swap)
    conv_width = 2 * conv_in.shape[2]
    conv_moves = (
        gathering(
            doubled(conv_shard[:, :conv_width], conv_swap.result[:, :conv_width]), cube.second
        ),
        gathering(
            doubled(conv_shard[:, conv_width:], conv_swap.result[:, conv_width:]), cube.first
        ),
    )
    pulled_near = jnp.stack([pick(pulled, item), pulled_swap.result])
    pulled_far = Move(once(pulled_near, "tp", 1))
    second_swap = across(ffn2_in), across(ffn2_out)
    anchor = issue(anchor, *attn_moves, *conv_moves, pulled_far, *second_swap)
    anchor = wait(anchor, *attn_moves)
    attn_weights = [move.result for move in attn_moves]
    mixed, attn_saved = attn_forward(attn_input, attn_weights[0])
    pair = Move(pair_sum(project_out(mixed, attn_weights[1])))
    anchor = wait(anchor, *conv_moves, pulled_far)
    anchor = fly(anchor, 2, *conv_moves)
    anchor = issue(anchor, pair)
    anchor = wait(anchor, pair)
    stream = stream + pair.result
    seed = whole_item(pulled_near, pulled_far.result)

    normed, conv_scaled, conv_inverse = normalize(stream, gains[2])
    conv_input = normed.astype(bf16)
    anchor = wait(anchor, *conv_moves)
    batch_pair = jnp.stack([batch_gain, batch_bias])
    batch_other = across(batch_pair)
    second_own = gathering(ffn2_in, cube.first), gathering(ffn2_out, cube.second)
    anchor = issue(anchor, *conv_moves, batch_other, *second_own)
    anchor = wait(anchor, *conv_moves, batch_other)
    batch_gain, batch_bias = jnp.concatenate([batch_pair, batch_other.result], axis=1)
    kernel_local = jnp.concatenate(
        [
            lax.dynamic_slice_in_dim(conv_kernel, start * channels, channels, 1)
            for start in (place, place ^ 2)
        ],
        axis=1,
    )
    conv_weights = [move.result for move in conv_moves]
    values_part, gate = value_gate(project_in(conv_input, conv_weights[0]))
    gated = values_part * jax.nn.sigmoid(gate)
    depthwise = depth_mix(kernel_local, gated, 1)
    masked_own = jnp.sum(pick(masked, item).astype(f32))
    sums = sum_items(
        jnp.stack(
            [
                jnp.sum(depthwise, axis=0),
                jnp.sum(depthwise * depthwise, axis=0),
                jnp.broadcast_to(masked_own, depthwise.shape[1:]),
            ]
        )
    )
    anchor = wait(anchor, *second_own, *second_swap)
    anchor = fly(anchor, 2, *second_own)
    masked_total = sums[2, 0]
    average = sums[0] / population
    variance = sums[1] / population - average * average
    batch_inverse = lax.rsqrt(variance + eps_batch)
    normal = (depthwise - average) * batch_inverse
    batched = normal * batch_gain + batch_bias
    conv_active = (batched * jax.nn.sigmoid(batched)).astype(bf16)
    conv_saved = values_part, gate, gated, normal, batch_inverse
    pair = Move(pair_sum(project_out(conv_active, conv_weights[1])))
    anchor = wait(anchor, *second_own)
    second_other = (
        gathering(second_swap[0].result, cube.first),
        gathering(second_swap[1].result, cube.second),
    )
    anchor = issue(anchor, pair, *second_own, *second_other)
    anchor = wait(anchor, pair)
    stream = stream + pair.result

    normed, second_scaled, second_inverse = normalize(stream, gains[3])
    second_input = normed.astype(bf16)
    anchor = wait(anchor, *second_other, *second_own)
    anchor = fly(anchor, 2, *second_other)
    second_weights = [[move.result for move in second_own]]
    partial_own, state = ffn_forward(second_input, *second_weights[0])
    second_states = [state]
    anchor = wait(anchor, *second_other)
    anchor = issue(anchor, *second_other)
    anchor = wait(anchor, *second_other)
    second_weights.append([move.result for move in second_other])
    partial_value, state = ffn_forward(second_input, *second_weights[1])
    second_states.append(state)
    pair = Move(pair_sum(partial_own + partial_value))
    anchor = issue(anchor, pair)
    anchor = wait(anchor, pair)
    stream = stream + 0.5 * pair.result
    final_out, final_scaled, final_inverse = normalize(stream, gains[4])

    def leaving(value):
        chunks = value.astype(bf16).reshape(parts, local_frames, width)
        both = jnp.concatenate([pick(chunks, place), pick(chunks, place ^ 2)], axis=0)
        both = mm(both, moved.astype(bf16), 1, 1)
        return both[:local_frames], across(both[local_frames:].astype(bf16))

    def landed(mine, move):
        other = move.result.astype(f32)
        return jnp.stack([jnp.where(item == 0, mine, other), jnp.where(item == 0, other, mine)])

    out_mine, out_move = leaving(final_out)
    grad_stream, gain_final = normalize_back(
        seed * jnp.sqrt(population / masked_total), final_scaled, final_inverse, gains[4]
    )
    whole_grad = (0.5 * grad_stream).astype(bf16)
    partial_value, second_hidden = 0.0, []
    for state, weights in zip(second_states, second_weights):
        part, grad_hidden = ffn_backward(whole_grad, state, *weights)
        partial_value = partial_value + part
        second_hidden.append(grad_hidden)
    pair = Move(pair_sum(partial_value))
    anchor = issue(anchor, pair)
    second_out = [
        (
            scattering(outer(second_input, second_hidden[quarter]), cube.first),
            scattering(outer(whole_grad, second_states[quarter][1]), cube.second),
        )
        for quarter in (0, 1)
    ]
    anchor = wait(anchor, pair)
    anchor = issue(anchor, *second_out[1], out_move)
    grad_local, gain_second = normalize_back(
        pair.result, second_scaled, second_inverse, gains[3]
    )
    grad_stream = grad_stream + grad_local

    whole_grad = grad_stream.astype(bf16)
    grad_batched = project_in(whole_grad, conv_weights[1]) * swish_slope(batched)
    grad_bias, grad_scale = sums = sum_items(
        jnp.stack([jnp.sum(grad_batched, axis=0), jnp.sum(grad_batched * normal, axis=0)])
    )
    anchor = wait(anchor, *second_out[1], out_move)
    anchor = issue(anchor, *second_out[1])
    grad_paired, kernel_part = conv_backward(
        grad_batched, sums, conv_saved, kernel_local, batch_gain, population
    )
    pair = Move(pair_sum(project_out(grad_paired, conv_weights[0])))
    anchor = wait(anchor, *second_out[1])
    anchor = fly(anchor, 1, *second_out[1])
    anchor = issue(anchor, pair, *second_out[0])
    conv_out_moves = (
        scattering(outer(conv_input, grad_paired), cube.second),
        scattering(outer(whole_grad, conv_active), cube.first),
    )
    anchor = wait(anchor, pair)
    grad_local, gain_conv = normalize_back(pair.result, conv_scaled, conv_inverse, gains[2])
    grad_stream = grad_stream + grad_local

    whole_grad = grad_stream.astype(bf16)
    anchor = wait(anchor, *second_out[1], *second_out[0])

    def crossing(moves):
        return across(jnp.concatenate([move.result.astype(bf16) for move in moves], axis=1))

    def crossing_half(moves):
        return across(
            jnp.concatenate([halves(move.result)[1].astype(bf16) for move in moves], axis=1)
        )

    second_back = crossing(second_out[1])
    anchor = issue(anchor, *second_out[0], second_back)
    grad_project = attn_backward(whole_grad, attn_saved, attn_weights[1])
    pair = Move(pair_sum(project_out(grad_project, attn_weights[0])))
    anchor = wait(anchor, *second_out[0])
    anchor = fly(anchor, 1, *second_out[0])
    anchor = issue(anchor, pair, *conv_out_moves)
    attn_out_moves = (
        scattering(outer(attn_input, grad_project), cube.first),
        scattering(outer(whole_grad, mixed), cube.second),
    )
    anchor = wait(anchor, pair)
    grad_local, gain_attn = normalize_back(pair.result, attn_scaled, attn_inverse, gains[1])
    grad_stream = grad_stream + grad_local

    whole_grad = (0.5 * grad_stream).astype(bf16)
    anchor = wait(anchor, *second_out[0], *conv_out_moves, second_back)
    anchor = issue(anchor, *conv_out_moves, *attn_out_moves)
    first_out = [None, None]
    partial_value = 0.0
    for quarter in (1, 0):
        part, grad_hidden = ffn_backward(
            whole_grad, first_states[quarter], *first_weights[quarter]
        )
        partial_value = partial_value + part
        first_out[quarter] = (
            scattering(outer(first_input, grad_hidden), cube.first),
            scattering(outer(whole_grad, first_states[quarter][1]), cube.second),
        )
    pair = Move(pair_sum(partial_value))
    anchor = wait(anchor, *conv_out_moves, *attn_out_moves)
    anchor = fly(anchor, 1, *conv_out_moves)
    anchor = issue(anchor, *first_out[1])
    anchor = wait(anchor, *first_out[1])
    anchor = issue(anchor, pair, *first_out[1])
    anchor = wait(anchor, *conv_out_moves)
    conv_back = crossing_half(conv_out_moves)
    anchor = wait(anchor, pair)
    grad_local, gain_first = normalize_back(pair.result, first_scaled, first_inverse, gains[0])
    grad_stream = grad_stream + grad_local
    mask_own = pick(masked, item)[:, None]
    feats_mine, feats_move = leaving(jnp.where(mask_own, 0.0, grad_stream))
    anchor = wait(anchor, *first_out[1])
    anchor = fly(anchor, 1, *first_out[1])
    anchor = issue(anchor, *first_out[0], feats_move)
    anchor = wait(anchor, *first_out[1], *first_out[0], feats_move)
    first_back = crossing(first_out[1])
    anchor = issue(anchor, first_back, *attn_out_moves)

    gain_grads = jnp.stack((gain_first, gain_attn, gain_conv, gain_second, gain_final))
    gain_grads = 0.5 * exact(gain_grads, 1)
    kernel_full = jnp.zeros(conv_kernel.shape, f32)
    for quarter, start in enumerate((place, place ^ 2)):
        kernel_full = lax.dynamic_update_slice_in_dim(
            kernel_full,
            kernel_part[:, quarter * channels : (quarter + 1) * channels],
            start * channels,
            1,
        )
    small = jnp.concatenate([gain_grads, kernel_full], axis=0)
    for bit in range(steps):
        small = small + swap(small, "dp", 1 << bit)
    small = small + swap(small, "tp", 2)
    small = small + swap(small, "tp", 1)
    norms = norm_gains.shape[0]

    anchor = wait(anchor, *attn_out_moves)
    anchor = fly(anchor, 1, *attn_out_moves)
    anchor = issue(anchor, conv_back)
    anchor = wait(anchor, *attn_out_moves)
    attn_back = crossing_half(attn_out_moves)
    anchor = issue(anchor, *first_out[0], attn_back)
    anchor = wait(anchor, *first_out[0])
    anchor = fly(anchor, 1, *first_out[0])
    anchor = wait(anchor, *first_out[0], first_back, conv_back, attn_back)

    def kept(moves, back, split):
        first, second = [halves(move.result)[0] if split else move.result for move in moves]
        other = back.result.astype(f32)
        return first + other[:, : first.shape[1]], second + other[:, first.shape[1] :]

    first_in_grad, first_out_grad = kept(first_out[0], first_back, False)
    second_in_grad, second_out_grad = kept(second_out[0], second_back, False)
    qkv_grad, attn_out_grad = kept(attn_out_moves, attn_back, True)
    conv_in_grad, conv_out_grad = kept(conv_out_moves, conv_back, True)
    return (
        landed(out_mine, out_move),
        landed(feats_mine, feats_move),
        masked_total,
        small[:norms],
        first_in_grad,
        first_out_grad,
        qkv_grad.reshape(qkv_weight.shape),
        attn_out_grad,
        conv_in_grad.reshape(conv_in.shape),
        small[norms:],
        grad_scale[:channels],
        grad_bias[:channels],
        conv_out_grad,
        second_in_grad,
        second_out_grad,
    )


def solution(mesh):
    return jax.shard_map(
        on_device,
        mesh=mesh,
        in_specs=(
            P("dp", "tp", None),
            P("dp", "tp", None),
            P("dp", None),
            P("dp"),
            P("dp", "tp", None),
            P(),
            P("dp", "tp"),
            P("dp", "tp"),
            P("dp", None, "tp"),
            P("dp", "tp"),
            P("dp", None, "tp"),
            P(),
            P("tp"),
            P("tp"),
            P("dp", "tp"),
            P("dp", "tp"),
            P("dp", "tp"),
        ),
        out_specs=(
            P("dp", "tp", None),
            P("dp", "tp", None),
            P(),
            P(),
            P("dp", "tp"),
            P("dp", "tp"),
            P("dp", None, "tp"),
            P("dp", "tp"),
            P("dp", None, "tp"),
            P(),
            P("tp"),
            P("tp"),
            P("dp", "tp"),
            P("dp", "tp"),
            P("dp", "tp"),
        ),
        check_vma=False,
    )
```
